256 devices in a mesh: space: 16 (over y, x), blk: 16 (over z, core).
Axes of the slice: x: 4, y: 4, z: 8, core: 2. Of those that a mesh axis runs over, the one named last changes fastest.
Arguments:
- snapshots: bfloat16 [64, 512, 3, 8192], P('blk', None, None, 'space'), may hold values from -6 to 6
- quadrature: float32 [8192], P('space'), may hold values from 0.2 to 5
- omega: float32 [16, 2, 64, 16], replicated, may hold values from -6 to 6
Outputs:
- modes: float32 [16, 2, 16, 3, 8192], P('blk', None, None, None, 'space')
- energies: float32 [16, 16], replicated
The draws below stay inside these ranges and needn't reach their ends.
All inputs are finite; a program needn't handle non-finite values.
Results may differ from the reference program's by a relative error of at most 0.0051.
Values may be sent and summed in bfloat16 or wider, within the bound.
A program may use at most 64 MiB of HBM per device.

```python
import math
import jax
import jax.numpy as jnp
from jax import lax

NT = 512
NF = 16
RANK = 16
COMP = 3
ITERS = 2
NS_STEPS = 14
POINTS = 8192
DOFS = 24576
BLOCKS = 64


def shard_levels(key, shape, split, least, high):
    loudness, own = 1.0, jax.random.fold_in(key, 6)
    for dim, blocks in split:
        steps = jnp.exp(jax.random.uniform(jax.random.fold_in(own, dim), (blocks,), jnp.float32, least / len(split), high / len(split)))
        loudness = loudness * jnp.repeat(steps, shape[dim] // blocks).reshape([-1 if axis == dim else 1 for axis in range(len(shape))])
    return loudness


def centred(rng, shape, width, limit, cuts=(), kind=jnp.bfloat16):
    array = jax.random.normal(rng, shape, jnp.float32) * width
    if len(cuts) > 0:
        array = shard_levels(rng, shape, cuts, -0.22, 0.18) * array
    return jnp.clip(array, min=-limit, max=limit).astype(kind)


def setup_inputs(seed: int = 0) -> dict:
    keys = jax.random.split(jax.random.key(seed), 4)
    snapshots = centred(keys[0], (BLOCKS, NT, COMP, POINTS), 1.0, 6.0, ((0, 16), (3, 16)))
    quadrature = jnp.clip(jnp.exp(math.log(5.0) - 3.218876 * jax.random.uniform(keys[1], (POINTS,), jnp.float32) ** shard_levels(keys[1], (POINTS,), ((0, 16),), -0.2, 0.2)), 0.2, 5.0)
    omega = centred(keys[2], (NF, 2, BLOCKS, RANK), 1.0, 6.0, (), jnp.float32)
    return dict(snapshots=snapshots, quadrature=quadrature, omega=omega)


def dft_table(sample_count, harmonic_count):
    sample = jnp.arange(sample_count, dtype=jnp.int32)
    harmonic = jnp.arange(1, harmonic_count + 1, dtype=jnp.int32)
    phase_turns = harmonic[:, None] * sample[None, :] % sample_count
    phases = 2.0 * math.pi / sample_count * phase_turns.astype(jnp.float32)
    ramp_angle = 2.0 * math.pi / sample_count * sample.astype(jnp.float32)
    window = 0.5 - 0.5 * jnp.cos(ramp_angle)
    factor = 1.0 / jnp.sqrt(jnp.sum(window * window))
    real_part = window * jnp.cos(phases) * factor
    imag_part = -window * jnp.sin(phases) * factor
    return jnp.concatenate([real_part, imag_part], 0).astype(jnp.bfloat16)

def batch_mm(left_mat, right_mat):
    return jnp.einsum('fab,fbc->fac', left_mat, right_mat, precision=lax.Precision.HIGHEST)

def cplx_mul(left_re, left_im, right_re, right_im):
    return (batch_mm(left_re, right_re) - batch_mm(left_im, right_im), batch_mm(left_re, right_im) + batch_mm(left_im, right_re))

def herm_mul(left_re, left_im, right_re, right_im):
    tl_re = jnp.swapaxes(left_re, 1, 2)
    tl_im = jnp.swapaxes(left_im, 1, 2)
    return (batch_mm(tl_re, right_re) + batch_mm(tl_im, right_im), batch_mm(tl_re, right_im) - batch_mm(tl_im, right_re))

def inverse_root(gram_re, gram_im):
    rank_count = gram_re.shape[-1]
    upper_half = jnp.concatenate([gram_re, -gram_im], -1)
    lower_half = jnp.concatenate([gram_im, gram_re], -1)
    joined = jnp.concatenate([upper_half, lower_half], -2)
    frob_norm = jnp.sqrt(lax.optimization_barrier(jnp.sum(joined * joined, axis=(1, 2))))[:, None, None]
    identity_mat = jnp.eye(2 * rank_count, dtype=jnp.float32)
    root_state = joined / frob_norm
    inverse_state = jnp.broadcast_to(identity_mat, joined.shape)
    for repeat_index in range(NS_STEPS):
        factor = 1.5 * identity_mat - 0.5 * batch_mm(inverse_state, root_state)
        root_state = batch_mm(root_state, factor)
        inverse_state = batch_mm(factor, inverse_state)
    inverse_state = inverse_state / jnp.sqrt(frob_norm)
    return (inverse_state[:, :rank_count, :rank_count], inverse_state[:, rank_count:, :rank_count])

def subspace(gram_re, gram_im, coef_re, coef_im):
    for repeat_index in range(ITERS):
        next_re, next_im = cplx_mul(gram_re, gram_im, coef_re, coef_im)
        image_re, image_im = cplx_mul(gram_re, gram_im, next_re, next_im)
        inner_re, inner_im = herm_mul(next_re, next_im, image_re, image_im)
        root_re, root_im = inverse_root(inner_re, inner_im)
        coef_re, coef_im = cplx_mul(next_re, next_im, root_re, root_im)
    final_re, final_im = cplx_mul(gram_re, gram_im, coef_re, coef_im)
    energies = lax.optimization_barrier(jnp.sum(final_re * final_re + final_im * final_im, axis=1))
    return (coef_re, coef_im, energies)

def reference(snapshots, quadrature, omega):
    kernel = dft_table(NT, NF)
    flattened = snapshots.reshape(BLOCKS, NT, DOFS)

    def one_block(one_snap):
        return jnp.dot(kernel, one_snap, preferred_element_type=jnp.float32)
    spectra = lax.map(one_block, flattened)
    root_weight = jnp.tile(jnp.sqrt(quadrature), COMP)
    weighted = (spectra * root_weight).astype(jnp.bfloat16)
    by_freq = jnp.transpose(weighted.reshape(BLOCKS, 2, NF, DOFS), (2, 1, 0, 3))

    def one_gram(freq_pair):
        re_rows = freq_pair[0]
        im_rows = freq_pair[1]
        rr_sum = jnp.dot(re_rows, re_rows.T, preferred_element_type=jnp.float32)
        ii_sum = jnp.dot(im_rows, im_rows.T, preferred_element_type=jnp.float32)
        ri_sum = jnp.dot(re_rows, im_rows.T, preferred_element_type=jnp.float32)
        ir_sum = jnp.dot(im_rows, re_rows.T, preferred_element_type=jnp.float32)
        return jnp.stack([rr_sum + ii_sum, ri_sum - ir_sum], 0)
    gram_matrix = lax.map(one_gram, by_freq) / DOFS
    coef_re, coef_im, energies = subspace(gram_matrix[:, 0], gram_matrix[:, 1], omega[:, 0], omega[:, 1])
    coef_low = jnp.stack([coef_re, coef_im], 1).astype(jnp.bfloat16)

    def one_mode(item_pair):
        freq_pair, coef_pair = item_pair
        re_rows = freq_pair[0]
        im_rows = freq_pair[1]
        coef_real = coef_pair[0].T
        coef_imag = coef_pair[1].T
        out_re = jnp.dot(coef_real, re_rows, preferred_element_type=jnp.float32) - jnp.dot(coef_imag, im_rows, preferred_element_type=jnp.float32)
        out_im = jnp.dot(coef_imag, re_rows, preferred_element_type=jnp.float32) + jnp.dot(coef_real, im_rows, preferred_element_type=jnp.float32)
        return jnp.stack([out_re, out_im], 0)
    modes = lax.map(one_mode, (by_freq, coef_low)) * (1.0 / root_weight)
    return (modes.reshape(NF, 2, RANK, COMP, POINTS), energies)
```

```python
import functools
import math

import jax
import jax.numpy as jnp
import numpy as np
from jax import lax
from jax.experimental import pallas as pl
from jax.experimental.pallas import tpu as pltpu
from jax.sharding import PartitionSpec as P

NT = 512
NF = 16
RANK = 16
COMP = 3
ITERS = 2
NS_STEPS = 14
SHARE = 4
ROWS = 2 * SHARE
HIGHEST = lax.Precision.HIGHEST
MESH = pl.DeviceIdType.MESH


def dft_table():
    sample = np.arange(NT)
    harmonic = np.arange(1, NF + 1)
    phases = 2.0 * math.pi / NT * (harmonic[:, None] * sample[None, :] % NT)
    window = 0.5 - 0.5 * np.cos(2.0 * math.pi / NT * sample)
    factor = 1.0 / np.sqrt(np.sum(window * window))
    table = np.concatenate([window * np.cos(phases), -window * np.sin(phases)], 0) * factor
    return table.astype(np.float32).astype(jnp.bfloat16)


def iota(shape, dim):
    return lax.broadcasted_iota(jnp.int32, shape, dim)


def mm(left, right, precision=HIGHEST):
    return jnp.dot(left, right, precision=precision, preferred_element_type=jnp.float32)


def mm_nt(left, right, precision=HIGHEST):
    return lax.dot_general(
        left, right, (((1,), (1,)), ((), ())), precision=precision, preferred_element_type=jnp.float32
    )


def pieces(value):
    high = value.astype(jnp.bfloat16).astype(jnp.float32)
    rest = value - high
    mid = rest.astype(jnp.bfloat16).astype(jnp.float32)
    return high, mid, rest - mid


def left_form(value):
    high, mid, low = pieces(value)
    lane = iota(value.shape, 1)
    near = jnp.where(lane < 96, high, mid).astype(jnp.bfloat16)
    far = jnp.where(lane < 32, mid, jnp.where(lane < 64, low, 0.0)).astype(jnp.bfloat16)
    return jnp.concatenate([near, far], axis=1)


def right_form(value):
    high, mid, low = (piece.astype(jnp.bfloat16) for piece in pieces(value))
    return jnp.concatenate([high, mid, low, high, mid, high, high, high], axis=0)


def wide(left, right):
    return jnp.dot(left, right, preferred_element_type=jnp.float32)


def inverse_root(joined):
    shape = joined.shape
    eye = jnp.where(iota(shape, 0) == iota(shape, 1) % (2 * RANK), 1.0, 0.0).astype(jnp.float32)
    squared = wide(left_form(joined), right_form(joined))
    own = jnp.where(iota(shape, 1) < 2 * RANK, joined * joined, 0.0)
    norm = jnp.sqrt(jnp.sum(jnp.sum(own, axis=0, keepdims=True), axis=1, keepdims=True))
    inv_norm = 1.0 / norm
    first = joined * inv_norm
    inverse_state = 1.5 * eye - 0.5 * first
    root_state = 1.5 * first - 0.5 * (squared * inv_norm * inv_norm)
    for step in range(1, NS_STEPS):
        factor = 1.5 * eye - 0.5 * wide(left_form(inverse_state), right_form(root_state))
        if step < NS_STEPS - 1:
            root_state = wide(left_form(root_state), right_form(factor))
        inverse_state = wide(left_form(factor), right_form(inverse_state))
    return inverse_state * (1.0 / jnp.sqrt(norm))


def kernel(
    groups,
    shares,
    snap_hbm,
    table_hbm,
    quad_hbm,
    omega_hbm,
    modes_hbm,
    energy_out,
    snap,
    table,
    quad,
    omega,
    filt,
    outgoing,
    spectra,
    gram_part,
    gram_in,
    gram,
    energy,
    modes,
    small_sem,
    load_sem,
    send_sem,
    recv_sem,
    gram_send,
    gram_recv,
    row_send,
    row_recv,
    energy_send,
    energy_recv,
    store_sem,
):
    group = lax.axis_index("blk")
    share = lax.axis_index("space")
    block_total = groups * SHARE
    lanes = groups * ROWS
    width = snap.shape[2]

    small = [
        pltpu.make_async_copy(table_hbm, table, small_sem.at[0]),
        pltpu.make_async_copy(quad_hbm, quad, small_sem.at[1]),
        pltpu.make_async_copy(omega_hbm.at[group], omega, small_sem.at[2]),
    ]
    for copy in small:
        copy.start()
    loads = [
        [
            pltpu.make_async_copy(snap_hbm.at[b, c], snap.at[c, pl.ds(b * NT, NT)], load_sem.at[c, b])
            for b in range(SHARE)
        ]
        for c in range(COMP)
    ]
    for per_comp in loads:
        for copy in per_comp:
            copy.start()

    barrier = pltpu.get_barrier_semaphore()

    def greet_group(i, carry):
        pl.semaphore_signal(
            barrier, inc=1, device_id=(share, lax.rem(group + i, groups)), device_id_type=MESH
        )
        return carry

    def greet_share(i, carry):
        pl.semaphore_signal(
            barrier, inc=1, device_id=(lax.rem(share + i, shares), group), device_id_type=MESH
        )
        return carry

    lax.fori_loop(1, groups, greet_group, 0)
    lax.fori_loop(1, shares, greet_share, 0)

    for copy in small:
        copy.wait()

    row = iota((lanes, 2 * NF), 0)
    column = iota((lanes, 2 * NF), 1)
    wanted = row // ROWS + NF * (row // SHARE % 2)
    for b in range(SHARE):
        chosen = jnp.where((column == wanted) & (row % SHARE == b), 1.0, 0.0).astype(jnp.bfloat16)
        filt[:, b * NT : (b + 1) * NT] = wide(chosen, table[...]).astype(jnp.bfloat16)
    root_weight = jnp.sqrt(quad[...])

    def block_copy(c, target):
        return pltpu.make_async_remote_copy(
            src_ref=outgoing.at[c, target],
            dst_ref=spectra.at[c, group],
            send_sem=send_sem.at[c],
            recv_sem=recv_sem.at[c],
            device_id=(share, target),
            device_id_type=MESH,
        )

    for c in range(COMP):
        for copy in loads[c]:
            copy.wait()
        weighted = (wide(filt[...], snap[c]) * root_weight).astype(jnp.bfloat16)
        outgoing[c] = weighted.reshape(groups, ROWS, width)
        if c == 0:
            pl.semaphore_wait(barrier, groups + shares - 2)

        def send_block(i, carry):
            block_copy(c, lax.rem(group + i, groups)).start()
            return carry

        lax.fori_loop(1, groups, send_block, 0)
        spectra[c, group] = outgoing[c, group]

    block = iota((block_total, lanes), 0)
    lane = iota((block_total, lanes), 1)
    same_block = block == lane // ROWS * SHARE + lane % SHARE
    is_real = lane // SHARE % 2 == 0
    real_lanes = jnp.where(same_block & is_real, 1.0, 0.0).astype(jnp.float32)
    imag_lanes = jnp.where(same_block & ~is_real, 1.0, 0.0).astype(jnp.float32)
    start_re, start_im = omega[0], omega[1]
    coef = mm(jnp.concatenate([start_re, start_im], 0), real_lanes) + mm(
        jnp.concatenate([-start_im, start_re], 0), imag_lanes
    )

    def whole(c):
        return spectra.at[c, pl.ds(0, groups - 1)]

    total = jnp.zeros((lanes, lanes), jnp.float32)
    for c in range(COMP):
        pltpu.make_async_remote_copy(
            src_ref=whole(c),
            dst_ref=whole(c),
            send_sem=send_sem.at[c],
            recv_sem=recv_sem.at[c],
            device_id=(share, lax.rem(group + 1, groups)),
            device_id_type=MESH,
        ).wait_recv()
        rows = spectra[c].reshape(lanes, width)
        total = total + mm_nt(rows, rows, None)

    gram_part[...] = total.reshape(shares, ROWS, lanes)

    def gram_copy(source, landing, peer, send, recv):
        return pltpu.make_async_remote_copy(
            src_ref=source,
            dst_ref=landing,
            send_sem=send,
            recv_sem=recv,
            device_id=(peer, group),
            device_id_type=MESH,
        )

    def send_part(i, carry):
        peer = lax.rem(share + i, shares)
        gram_copy(gram_part.at[peer], gram_in.at[share], peer, gram_send, gram_recv).start()
        return carry

    lax.fori_loop(1, shares, send_part, 0)
    gram_in[share] = gram_part[share]
    others = pl.ds(0, shares - 1)
    next_share = lax.rem(share + 1, shares)
    gram_copy(gram_in.at[others], gram_in.at[others], next_share, gram_send, gram_recv).wait_recv()
    mine = jnp.sum(gram_in[...], axis=0)
    rolled = pltpu.roll(mine, SHARE, 0)
    lane = iota((ROWS, lanes), 1) // SHARE % 2
    partner = jnp.where(
        lane == 0, pltpu.roll(rolled, lanes - SHARE, 1), pltpu.roll(rolled, SHARE, 1)
    )
    partner = jnp.where(lane == iota((ROWS, lanes), 0) // SHARE, partner, -partner)
    gram[share] = (mine + partner) * (1.0 / (COMP * width * shares))

    def send_row(i, carry):
        gram_copy(gram.at[share], gram.at[share], lax.rem(share + i, shares), row_send, row_recv).start()
        return carry

    lax.fori_loop(1, shares, send_row, 0)
    gram_copy(gram.at[others], gram.at[others], next_share, row_send, row_recv).wait_recv()
    matrix = gram[...].reshape(lanes, lanes)

    nxt = mm(coef, matrix)
    image = mm(nxt, matrix)
    for step in range(ITERS):
        joined = mm_nt(nxt, jnp.concatenate([image] * 4, 0))
        if step < ITERS - 1:
            further = mm(image, matrix)
            left = left_form(inverse_root(joined))
            nxt, image = wide(left, right_form(image)), wide(left, right_form(further))
        else:
            left = left_form(inverse_root(joined))
            coef, final = wide(left, right_form(nxt)), wide(left, right_form(image))

    squares = mm_nt(jnp.ones((ROWS, lanes), jnp.float32), jnp.concatenate([final * final] * 4, 0))
    energy[group] = squares[:1, :]

    def energy_copy(source, landing, peer):
        return pltpu.make_async_remote_copy(
            src_ref=source,
            dst_ref=landing,
            send_sem=energy_send,
            recv_sem=energy_recv,
            device_id=(share, peer),
            device_id_type=MESH,
        )

    def send_energy(i, carry):
        energy_copy(energy.at[group], energy.at[group], lax.rem(group + i, groups)).start()
        return carry

    lax.fori_loop(1, groups, send_energy, 0)

    coef_low = coef.astype(jnp.bfloat16)
    inv_weight = 1.0 / root_weight
    for c in range(COMP):
        out = wide(coef_low, spectra[c].reshape(lanes, width)) * inv_weight
        modes[0, c] = out[:RANK]
        modes[1, c] = out[RANK:]
    store = pltpu.make_async_copy(modes, modes_hbm, store_sem)
    store.start()

    other_groups = pl.ds(0, groups - 1)
    next_group = lax.rem(group + 1, groups)
    energy_copy(energy.at[other_groups], energy.at[other_groups], next_group).wait()
    energy_out[...] = energy[...].reshape(groups, 128)[:, :RANK]
    gram_copy(gram_in.at[others], gram_in.at[others], next_share, gram_send, gram_recv).wait_send()
    gram_copy(gram.at[others], gram.at[others], next_share, row_send, row_recv).wait_send()
    for c in range(COMP):
        pltpu.make_async_remote_copy(
            src_ref=whole(c),
            dst_ref=whole(c),
            send_sem=send_sem.at[c],
            recv_sem=recv_sem.at[c],
            device_id=(share, next_group),
            device_id_type=MESH,
        ).wait_send()
    store.wait()


def per_device(snapshots, quadrature, omega):
    groups, shares = lax.axis_size("blk"), lax.axis_size("space")
    width = snapshots.shape[3]
    lanes = groups * ROWS
    any_space = pl.BlockSpec(memory_space=pl.ANY)
    dma = pltpu.SemaphoreType.DMA
    modes, energies = pl.pallas_call(
        functools.partial(kernel, groups, shares),
        out_shape=(
            jax.ShapeDtypeStruct((2, COMP, RANK, width), jnp.float32),
            jax.ShapeDtypeStruct((NF, RANK), jnp.float32),
        ),
        in_specs=[any_space] * 4,
        out_specs=(any_space, pl.BlockSpec(memory_space=pltpu.VMEM)),
        scratch_shapes=[
            pltpu.VMEM((COMP, SHARE * NT, width), jnp.bfloat16),
            pltpu.VMEM((2 * NF, NT), jnp.bfloat16),
            pltpu.VMEM((1, width), jnp.float32),
            pltpu.VMEM((2, RANK, groups * SHARE), jnp.float32),
            pltpu.VMEM((lanes, SHARE * NT), jnp.bfloat16),
            pltpu.VMEM((COMP, groups, ROWS, width), jnp.bfloat16),
            pltpu.VMEM((COMP, groups, ROWS, width), jnp.bfloat16),
            pltpu.VMEM((shares, ROWS, lanes), jnp.float32),
            pltpu.VMEM((shares, ROWS, lanes), jnp.float32),
            pltpu.VMEM((shares, ROWS, lanes), jnp.float32),
            pltpu.VMEM((groups, 1, 128), jnp.float32),
            pltpu.VMEM((2, COMP, RANK, width), jnp.float32),
            dma((3,)),
            dma((COMP, SHARE)),
            dma((COMP,)),
            dma((COMP,)),
            dma(()),
            dma(()),
            dma(()),
            dma(()),
            dma(()),
            dma(()),
            dma(()),
        ],
        compiler_params=pltpu.CompilerParams(
            collective_id=0, has_side_effects=True, vmem_limit_bytes=40 << 20
        ),
    )(
        jnp.transpose(snapshots, (0, 2, 1, 3)),
        jnp.asarray(dft_table()),
        quadrature.reshape(1, width),
        jnp.transpose(omega, (0, 1, 3, 2)),
    )
    return jnp.transpose(modes, (0, 2, 1, 3))[None], energies


def solution(mesh):
    in_specs = (P("blk", None, None, "space"), P("space"), P())
    out_specs = (P("blk", None, None, None, "space"), P())
    return jax.shard_map(
        per_device, mesh=mesh, in_specs=in_specs, out_specs=out_specs, check_vma=False
    )
```

```python
import functools
import math

import jax
import jax.numpy as jnp
import numpy as np
from jax import lax
from jax.experimental import pallas as pl
from jax.experimental.pallas import tpu as pltpu
from jax.sharding import PartitionSpec as P

NT = 512
NF = 16
RANK = 16
COMP = 3
ITERS = 2
NS_STEPS = 14
SHARE = 4
ROWS = 2 * SHARE
HIGHEST = lax.Precision.HIGHEST
MESH = pl.DeviceIdType.MESH


def dft_table():
    sample = np.arange(NT)
    harmonic = np.arange(1, NF + 1)
    phases = 2.0 * math.pi / NT * (harmonic[:, None] * sample[None, :] % NT)
    window = 0.5 - 0.5 * np.cos(2.0 * math.pi / NT * sample)
    factor = 1.0 / np.sqrt(np.sum(window * window))
    table = np.concatenate([window * np.cos(phases), -window * np.sin(phases)], 0) * factor
    return table.astype(np.float32).astype(jnp.bfloat16)


def far_first(count):
    return sorted(range(1, count), key=lambda step: -min(step, count - step))


def grid_far_first(side):
    offsets = [(i, j) for i in range(side) for j in range(side) if i or j]
    return sorted(offsets, key=lambda o: -min(o[0], side - o[0]) - min(o[1], side - o[1]))


def iota(shape, dim):
    return lax.broadcasted_iota(jnp.int32, shape, dim)


def mm(left, right, precision=HIGHEST):
    return jnp.dot(left, right, precision=precision, preferred_element_type=jnp.float32)


def mm_nt(left, right, precision=HIGHEST):
    return lax.dot_general(
        left, right, (((1,), (1,)), ((), ())), precision=precision, preferred_element_type=jnp.float32
    )


def pieces(value):
    high = value.astype(jnp.bfloat16).astype(jnp.float32)
    rest = value - high
    mid = rest.astype(jnp.bfloat16).astype(jnp.float32)
    return high, mid, rest - mid


def left_form(value):
    high, mid, low = pieces(value)
    lane = iota(value.shape, 1)
    near = jnp.where(lane < 96, high, mid).astype(jnp.bfloat16)
    far = jnp.where(lane < 32, mid, jnp.where(lane < 64, low, 0.0)).astype(jnp.bfloat16)
    return jnp.concatenate([near, far], axis=1)


def right_form(value):
    high, mid, low = (piece.astype(jnp.bfloat16) for piece in pieces(value))
    return jnp.concatenate([high, mid, low, high, mid, high, high, high], axis=0)


def wide(left, right):
    return jnp.dot(left, right, preferred_element_type=jnp.float32)


def lane_sum_free(value):
    for shift in (4, 2, 1):
        value = value + pltpu.roll(value, shift, 0)
    return value


def take(value, index):
    return jnp.take_along_axis(value, index, axis=1)


class Flat:
    def __init__(self):
        sub, lane = iota((8, 128), 0), iota((8, 128), 1)
        self.left_index = [lane // RANK * RANK + 8 * half + sub for half in range(2)]
        self.right_index = sub * RANK + lane % RANK
        self.own_row = lane // RANK == sub
        zero = jnp.zeros((8, 128), jnp.float32)
        self.eye = [
            jnp.where(lane // RANK + 8 * half == lane % RANK, 1.0, 0.0).astype(jnp.float32)
            for half in range(2)
        ] + [zero, zero]

    def left(self, mat):
        return [[[take(mat[2 * p + h], self.left_index[k]) for k in range(2)] for h in range(2)] for p in range(2)]

    def right(self, mat):
        return [[take(mat[2 * p + k], self.right_index) for k in range(2)] for p in range(2)]

    def product(self, left, right):
        out = []
        for p in range(2):
            for h in range(2):
                if p == 0:
                    terms = [left[0][h][k] * right[0][k] - left[1][h][k] * right[1][k] for k in range(2)]
                else:
                    terms = [left[0][h][k] * right[1][k] + left[1][h][k] * right[0][k] for k in range(2)]
                out.append(lane_sum_free(terms[0] + terms[1]))
        return out

    def from_rows(self, rows):
        return [
            lane_sum_free(jnp.where(self.own_row, rows[8 * part : 8 * part + 8], 0.0))
            for part in range(4)
        ]

    def embedded(self, mat):
        real = jnp.concatenate([take(mat[0], self.right_index), take(mat[1], self.right_index)], 0)
        imag = jnp.concatenate([take(mat[2], self.right_index), take(mat[3], self.right_index)], 0)
        first = iota((RANK, 128), 1) % (2 * RANK) < RANK
        return jnp.concatenate([jnp.where(first, real, -imag), jnp.where(first, imag, real)], 0)

    def inverse_root(self, mat):
        eye = self.eye
        square = sum(entry * entry for entry in mat)
        norm = jnp.sqrt(2.0 * jnp.sum(square, axis=1, keepdims=True))
        inv_norm = 1.0 / norm
        squared = self.product(self.left(mat), self.right(mat))
        first = [entry * inv_norm for entry in mat]
        inverse_state = [1.5 * one - 0.5 * entry for one, entry in zip(eye, first)]
        root_state = [
            1.5 * entry - 0.5 * (twice * (inv_norm * inv_norm)) for entry, twice in zip(first, squared)
        ]
        for step in range(1, NS_STEPS):
            both = self.product(self.left(inverse_state), self.right(root_state))
            factor = [1.5 * one - 0.5 * entry for one, entry in zip(eye, both)]
            inverse_state = self.product(self.left(factor), self.right(inverse_state))
            if step < NS_STEPS - 1:
                root_state = self.product(self.left(root_state), self.right(factor))
        scale = 1.0 / jnp.sqrt(norm)
        return [entry * scale for entry in inverse_state]


def kernel(
    groups,
    shares,
    snap_hbm,
    table_hbm,
    quad_hbm,
    omega_hbm,
    modes_hbm,
    energy_out,
    snap,
    table,
    quad,
    omega,
    filt,
    outgoing,
    spectra,
    gram_part,
    gram_in,
    gram,
    energy,
    modes,
    small_sem,
    load_sem,
    send_sem,
    recv_sem,
    gram_send,
    gram_recv,
    row_send,
    row_recv,
    energy_send,
    energy_recv,
    store_sem,
):
    group = lax.axis_index("blk")
    share = lax.axis_index("space")
    block_total = groups * SHARE
    lanes = groups * ROWS
    width = snap.shape[2]

    small = [
        pltpu.make_async_copy(table_hbm, table, small_sem.at[0]),
        pltpu.make_async_copy(quad_hbm, quad, small_sem.at[1]),
        pltpu.make_async_copy(omega_hbm.at[group], omega, small_sem.at[2]),
    ]
    for copy in small:
        copy.start()
    loads = [
        [
            pltpu.make_async_copy(snap_hbm.at[b, c], snap.at[c, pl.ds(b * NT, NT)], load_sem.at[c, b])
            for b in range(SHARE)
        ]
        for c in range(COMP)
    ]
    for per_comp in loads[:2]:
        for copy in per_comp:
            copy.start()

    barrier = pltpu.get_barrier_semaphore()

    def greet_group(i, carry):
        pl.semaphore_signal(
            barrier, inc=1, device_id=(share, lax.rem(group + i, groups)), device_id_type=MESH
        )
        return carry

    def greet_share(i, carry):
        pl.semaphore_signal(
            barrier, inc=1, device_id=(lax.rem(share + i, shares), group), device_id_type=MESH
        )
        return carry

    lax.fori_loop(1, groups, greet_group, 0)
    lax.fori_loop(1, shares, greet_share, 0)

    for copy in small:
        copy.wait()

    row = iota((lanes, 2 * NF), 0)
    column = iota((lanes, 2 * NF), 1)
    wanted = row // ROWS + NF * (row // SHARE % 2)
    for b in range(SHARE):
        chosen = jnp.where((column == wanted) & (row % SHARE == b), 1.0, 0.0).astype(jnp.bfloat16)
        filt[:, b * NT : (b + 1) * NT] = wide(chosen, table[...]).astype(jnp.bfloat16)
    root_weight = jnp.sqrt(quad[...])

    def block_copy(c, target):
        return pltpu.make_async_remote_copy(
            src_ref=outgoing.at[c, target],
            dst_ref=spectra.at[c, group],
            send_sem=send_sem.at[c],
            recv_sem=recv_sem.at[c],
            device_id=(share, target),
            device_id_type=MESH,
        )

    for c in range(COMP):
        for copy in loads[c]:
            copy.wait()
        if c + 2 < COMP:
            for copy in loads[c + 2]:
                copy.start()
        weighted = (wide(filt[...], snap[c]) * root_weight).astype(jnp.bfloat16)
        outgoing[c] = weighted.reshape(groups, ROWS, width)
        if c == 0:
            pl.semaphore_wait(barrier, groups + shares - 2)

        for i in far_first(groups):
            block_copy(c, lax.rem(group + i, groups)).start()
        spectra[c, group] = outgoing[c, group]

    block = iota((block_total, lanes), 0)
    lane = iota((block_total, lanes), 1)
    same_block = block == lane // ROWS * SHARE + lane % SHARE
    is_real = lane // SHARE % 2 == 0
    real_lanes = jnp.where(same_block & is_real, 1.0, 0.0).astype(jnp.float32)
    imag_lanes = jnp.where(same_block & ~is_real, 1.0, 0.0).astype(jnp.float32)
    start_re, start_im = omega[0], omega[1]
    coef = mm(jnp.concatenate([start_re, start_im], 0), real_lanes) + mm(
        jnp.concatenate([-start_im, start_re], 0), imag_lanes
    )

    def whole(c):
        return spectra.at[c, pl.ds(0, groups - 1)]

    total = jnp.zeros((lanes, lanes), jnp.float32)
    for c in range(COMP):
        pltpu.make_async_remote_copy(
            src_ref=whole(c),
            dst_ref=whole(c),
            send_sem=send_sem.at[c],
            recv_sem=recv_sem.at[c],
            device_id=(share, lax.rem(group + 1, groups)),
            device_id_type=MESH,
        ).wait_recv()
        rows = spectra[c].reshape(lanes, width)
        total = total + mm_nt(rows, rows, None)

    gram_part[...] = total.reshape(shares, ROWS, lanes)

    def gram_copy(source, landing, peer, send, recv):
        return pltpu.make_async_remote_copy(
            src_ref=source,
            dst_ref=landing,
            send_sem=send,
            recv_sem=recv,
            device_id=(peer, group),
            device_id_type=MESH,
        )

    side = math.isqrt(shares)
    peers = [
        lax.rem(share // side + i, side) * side + lax.rem(share + j, side)
        for i, j in grid_far_first(side)
    ]
    for peer in peers:
        gram_copy(gram_part.at[peer], gram_in.at[share], peer, gram_send, gram_recv).start()
    gram_in[share] = gram_part[share]
    others = pl.ds(0, shares - 1)
    next_share = lax.rem(share + 1, shares)
    gram_copy(gram_in.at[others], gram_in.at[others], next_share, gram_send, gram_recv).wait_recv()
    mine = jnp.sum(gram_in[...], axis=0)
    rolled = pltpu.roll(mine, SHARE, 0)
    lane = iota((ROWS, lanes), 1) // SHARE % 2
    partner = jnp.where(
        lane == 0, pltpu.roll(rolled, lanes - SHARE, 1), pltpu.roll(rolled, SHARE, 1)
    )
    partner = jnp.where(lane == iota((ROWS, lanes), 0) // SHARE, partner, -partner)
    gram[share] = (mine + partner) * (1.0 / (COMP * width * shares))

    for peer in peers:
        gram_copy(gram.at[share], gram.at[share], peer, row_send, row_recv).start()
    gram_copy(gram.at[others], gram.at[others], next_share, row_send, row_recv).wait_recv()
    matrix = gram[...].reshape(lanes, lanes)

    nxt = mm(coef, matrix)
    image = mm(nxt, matrix)
    flat = Flat()
    for step in range(ITERS):
        rows = mm_nt(nxt, jnp.concatenate([image[:RANK]] * 8, 0))
        if step < ITERS - 1:
            further = mm(image, matrix)
        left = left_form(flat.embedded(flat.inverse_root(flat.from_rows(rows))))
        if step < ITERS - 1:
            nxt, image = wide(left, right_form(image)), wide(left, right_form(further))
        else:
            coef, final = wide(left, right_form(nxt)), wide(left, right_form(image))

    squares = mm_nt(jnp.ones((ROWS, lanes), jnp.float32), jnp.concatenate([final * final] * 4, 0))
    energy[group] = squares[:1, :]

    def energy_copy(source, landing, peer):
        return pltpu.make_async_remote_copy(
            src_ref=source,
            dst_ref=landing,
            send_sem=energy_send,
            recv_sem=energy_recv,
            device_id=(share, peer),
            device_id_type=MESH,
        )

    for i in far_first(groups):
        energy_copy(energy.at[group], energy.at[group], lax.rem(group + i, groups)).start()

    coef_low = coef.astype(jnp.bfloat16)
    inv_weight = 1.0 / root_weight
    for c in range(COMP):
        out = wide(coef_low, spectra[c].reshape(lanes, width)) * inv_weight
        modes[0, c] = out[:RANK]
        modes[1, c] = out[RANK:]
    store = pltpu.make_async_copy(modes, modes_hbm, store_sem)
    store.start()

    other_groups = pl.ds(0, groups - 1)
    next_group = lax.rem(group + 1, groups)
    energy_copy(energy.at[other_groups], energy.at[other_groups], next_group).wait()
    energy_out[...] = energy[...].reshape(groups, 128)[:, :RANK]
    gram_copy(gram_in.at[others], gram_in.at[others], next_share, gram_send, gram_recv).wait_send()
    gram_copy(gram.at[others], gram.at[others], next_share, row_send, row_recv).wait_send()
    for c in range(COMP):
        pltpu.make_async_remote_copy(
            src_ref=whole(c),
            dst_ref=whole(c),
            send_sem=send_sem.at[c],
            recv_sem=recv_sem.at[c],
            device_id=(share, next_group),
            device_id_type=MESH,
        ).wait_send()
    store.wait()


def per_device(snapshots, quadrature, omega):
    groups, shares = lax.axis_size("blk"), lax.axis_size("space")
    width = snapshots.shape[3]
    lanes = groups * ROWS
    any_space = pl.BlockSpec(memory_space=pl.ANY)
    dma = pltpu.SemaphoreType.DMA
    modes, energies = pl.pallas_call(
        functools.partial(kernel, groups, shares),
        out_shape=(
            jax.ShapeDtypeStruct((2, COMP, RANK, width), jnp.float32),
            jax.ShapeDtypeStruct((NF, RANK), jnp.float32),
        ),
        in_specs=[any_space] * 4,
        out_specs=(any_space, pl.BlockSpec(memory_space=pltpu.VMEM)),
        scratch_shapes=[
            pltpu.VMEM((COMP, SHARE * NT, width), jnp.bfloat16),
            pltpu.VMEM((2 * NF, NT), jnp.bfloat16),
            pltpu.VMEM((1, width), jnp.float32),
            pltpu.VMEM((2, RANK, groups * SHARE), jnp.float32),
            pltpu.VMEM((lanes, SHARE * NT), jnp.bfloat16),
            pltpu.VMEM((COMP, groups, ROWS, width), jnp.bfloat16),
            pltpu.VMEM((COMP, groups, ROWS, width), jnp.bfloat16),
            pltpu.VMEM((shares, ROWS, lanes), jnp.float32),
            pltpu.VMEM((shares, ROWS, lanes), jnp.float32),
            pltpu.VMEM((shares, ROWS, lanes), jnp.float32),
            pltpu.VMEM((groups, 1, 128), jnp.float32),
            pltpu.VMEM((2, COMP, RANK, width), jnp.float32),
            dma((3,)),
            dma((COMP, SHARE)),
            dma((COMP,)),
            dma((COMP,)),
            dma(()),
            dma(()),
            dma(()),
            dma(()),
            dma(()),
            dma(()),
            dma(()),
        ],
        compiler_params=pltpu.CompilerParams(
            collective_id=0, has_side_effects=True, vmem_limit_bytes=40 << 20
        ),
    )(
        *(
            pltpu.with_memory_space_constraint(operand, pltpu.HBM)
            for operand in (
                jnp.transpose(snapshots, (0, 2, 1, 3)),
                jnp.asarray(dft_table()),
                quadrature.reshape(1, width),
                jnp.transpose(omega, (0, 1, 3, 2)),
            )
        )
    )
    return jnp.transpose(modes, (0, 2, 1, 3))[None], energies


def solution(mesh):
    in_specs = (P("blk", None, None, "space"), P("space"), P())
    out_specs = (P("blk", None, None, None, "space"), P())
    return jax.shard_map(
        per_device, mesh=mesh, in_specs=in_specs, out_specs=out_specs, check_vma=False
    )
```

```python
import functools
import math

import jax
import jax.numpy as jnp
import numpy as np
from jax import lax
from jax.experimental import pallas as pl
from jax.experimental.pallas import tpu as pltpu
from jax.sharding import PartitionSpec as P

NT = 512
NF = 16
RANK = 16
COMP = 3
ITERS = 2
NS_STEPS = 14
SHARE = 4
ROWS = 2 * SHARE
PARTS = ((0, 1), (1, 2))
HIGHEST = lax.Precision.HIGHEST
MESH = pl.DeviceIdType.MESH


def dft_table():
    sample = np.arange(NT)
    harmonic = np.arange(1, NF + 1)
    phases = 2.0 * math.pi / NT * (harmonic[:, None] * sample[None, :] % NT)
    window = 0.5 - 0.5 * np.cos(2.0 * math.pi / NT * sample)
    factor = 1.0 / np.sqrt(np.sum(window * window))
    table = np.concatenate([window * np.cos(phases), -window * np.sin(phases)], 0) * factor
    return table.astype(np.float32).astype(jnp.bfloat16)


def far_first(count):
    return sorted(range(1, count), key=lambda step: -min(step, count - step))


def grid_far_first(side):
    offsets = [(i, j) for i in range(side) for j in range(side) if i or j]
    return sorted(offsets, key=lambda o: -min(o[0], side - o[0]) - min(o[1], side - o[1]))


def iota(shape, dim):
    return lax.broadcasted_iota(jnp.int32, shape, dim)


def mm(left, right, precision=HIGHEST):
    return jnp.dot(left, right, precision=precision, preferred_element_type=jnp.float32)


def mm_nt(left, right, precision=HIGHEST):
    return lax.dot_general(
        left, right, (((1,), (1,)), ((), ())), precision=precision, preferred_element_type=jnp.float32
    )


def pieces(value):
    high = value.astype(jnp.bfloat16).astype(jnp.float32)
    rest = value - high
    mid = rest.astype(jnp.bfloat16).astype(jnp.float32)
    return high, mid, rest - mid


def left_form(value):
    high, mid, low = pieces(value)
    lane = iota(value.shape, 1)
    near = jnp.where(lane < 96, high, mid).astype(jnp.bfloat16)
    far = jnp.where(lane < 32, mid, jnp.where(lane < 64, low, 0.0)).astype(jnp.bfloat16)
    return jnp.concatenate([near, far], axis=1)


def right_form(value):
    high, mid, low = (piece.astype(jnp.bfloat16) for piece in pieces(value))
    return jnp.concatenate([high, mid, low, high, mid, high, high, high], axis=0)


def wide(left, right):
    return jnp.dot(left, right, preferred_element_type=jnp.float32)


def lane_sum_free(value):
    for shift in (4, 2, 1):
        value = value + pltpu.roll(value, shift, 0)
    return value


def take(value, index):
    return jnp.take_along_axis(value, index, axis=1)


class Flat:
    def __init__(self):
        sub, lane = iota((8, 128), 0), iota((8, 128), 1)
        self.left_index = [lane // RANK * RANK + 8 * half + sub for half in range(2)]
        self.right_index = sub * RANK + lane % RANK
        self.own_row = lane // RANK == sub
        zero = jnp.zeros((8, 128), jnp.float32)
        self.eye = [
            jnp.where(lane // RANK + 8 * half == lane % RANK, 1.0, 0.0).astype(jnp.float32)
            for half in range(2)
        ] + [zero, zero]

    def left(self, mat):
        return [[[take(mat[2 * p + h], self.left_index[k]) for k in range(2)] for h in range(2)] for p in range(2)]

    def right(self, mat):
        return [[take(mat[2 * p + k], self.right_index) for k in range(2)] for p in range(2)]

    def product(self, left, right):
        out = []
        for p in range(2):
            for h in range(2):
                if p == 0:
                    terms = [left[0][h][k] * right[0][k] - left[1][h][k] * right[1][k] for k in range(2)]
                else:
                    terms = [left[0][h][k] * right[1][k] + left[1][h][k] * right[0][k] for k in range(2)]
                out.append(lane_sum_free(terms[0] + terms[1]))
        return out

    def from_rows(self, rows):
        return [
            lane_sum_free(jnp.where(self.own_row, rows[8 * part : 8 * part + 8], 0.0))
            for part in range(4)
        ]

    def embedded(self, mat):
        real = jnp.concatenate([take(mat[0], self.right_index), take(mat[1], self.right_index)], 0)
        imag = jnp.concatenate([take(mat[2], self.right_index), take(mat[3], self.right_index)], 0)
        first = iota((RANK, 128), 1) % (2 * RANK) < RANK
        return jnp.concatenate([jnp.where(first, real, -imag), jnp.where(first, imag, real)], 0)

    def inverse_root(self, mat):
        eye = self.eye
        square = sum(entry * entry for entry in mat)
        norm = jnp.sqrt(2.0 * jnp.sum(square, axis=1, keepdims=True))
        inv_norm = 1.0 / norm
        squared = self.product(self.left(mat), self.right(mat))
        first = [entry * inv_norm for entry in mat]
        inverse_state = [1.5 * one - 0.5 * entry for one, entry in zip(eye, first)]
        root_state = [
            1.5 * entry - 0.5 * (twice * (inv_norm * inv_norm)) for entry, twice in zip(first, squared)
        ]
        for step in range(1, NS_STEPS):
            both = self.product(self.left(inverse_state), self.right(root_state))
            factor = [1.5 * one - 0.5 * entry for one, entry in zip(eye, both)]
            inverse_state = self.product(self.left(factor), self.right(inverse_state))
            if step < NS_STEPS - 1:
                root_state = self.product(self.left(root_state), self.right(factor))
        scale = 1.0 / jnp.sqrt(norm)
        return [entry * scale for entry in inverse_state]


def kernel(
    groups,
    shares,
    snap_hbm,
    table_hbm,
    quad_hbm,
    omega_hbm,
    modes_hbm,
    energy_out,
    snap,
    table,
    quad,
    omega,
    filt,
    outgoing,
    spectra,
    gram_in,
    energy,
    modes,
    small_sem,
    load_sem,
    send_sem,
    recv_sem,
    gram_send,
    gram_recv,
    energy_send,
    energy_recv,
    store_sem,
):
    group = lax.axis_index("blk")
    share = lax.axis_index("space")
    block_total = groups * SHARE
    lanes = groups * ROWS
    width = snap.shape[2]

    barrier = pltpu.get_barrier_semaphore()
    side = math.isqrt(shares)
    group_peers = [lax.rem(group + i, groups) for i in far_first(groups)]
    share_peers = [
        lax.rem(share // side + i, side) * side + lax.rem(share + j, side)
        for i, j in grid_far_first(side)
    ]
    for peer in group_peers:
        pl.semaphore_signal(barrier, inc=1, device_id=(share, peer), device_id_type=MESH)
    for peer in share_peers:
        pl.semaphore_signal(barrier, inc=1, device_id=(peer, group), device_id_type=MESH)

    small = [
        pltpu.make_async_copy(table_hbm, table, small_sem.at[0]),
        pltpu.make_async_copy(quad_hbm, quad, small_sem.at[1]),
        pltpu.make_async_copy(omega_hbm.at[group], omega, small_sem.at[2]),
    ]
    for copy in small:
        copy.start()
    loads = [
        [
            pltpu.make_async_copy(snap_hbm.at[b, c], snap.at[c, pl.ds(b * NT, NT)], load_sem.at[c, b])
            for b in range(SHARE)
        ]
        for c in range(COMP)
    ]
    for per_comp in loads:
        for copy in per_comp:
            copy.start()


    for copy in small:
        copy.wait()

    row = iota((lanes, 2 * NF), 0)
    column = iota((lanes, 2 * NF), 1)
    wanted = row // ROWS + NF * (row // SHARE % 2)
    for b in range(SHARE):
        chosen = jnp.where((column == wanted) & (row % SHARE == b), 1.0, 0.0).astype(jnp.bfloat16)
        filt[:, b * NT : (b + 1) * NT] = wide(chosen, table[...]).astype(jnp.bfloat16)
    root_weight = jnp.sqrt(quad[...])

    def block_copy(part, source, landing, peer):
        return pltpu.make_async_remote_copy(
            src_ref=source,
            dst_ref=landing,
            send_sem=send_sem.at[part],
            recv_sem=recv_sem.at[part],
            device_id=(share, peer),
            device_id_type=MESH,
        )

    for c in range(COMP):
        for copy in loads[c]:
            copy.wait()
        weighted = (wide(filt[...], snap[c]) * root_weight).astype(jnp.bfloat16)
        outgoing[:, c] = weighted.reshape(groups, ROWS, width)
        for part, (begin, count) in enumerate(PARTS):
            if c != begin + count - 1:
                continue
            if part == 0:
                pl.semaphore_wait(barrier, groups + shares - 2)
            comps = pl.ds(begin, count)
            for peer in group_peers:
                block_copy(part, outgoing.at[peer, comps], spectra.at[group, comps], peer).start()
    spectra[group] = outgoing[group]

    block = iota((block_total, lanes), 0)
    lane = iota((block_total, lanes), 1)
    same_block = block == lane // ROWS * SHARE + lane % SHARE
    is_real = lane // SHARE % 2 == 0
    real_lanes = jnp.where(same_block & is_real, 1.0, 0.0).astype(jnp.float32)
    imag_lanes = jnp.where(same_block & ~is_real, 1.0, 0.0).astype(jnp.float32)
    start_re, start_im = omega[0], omega[1]
    coef = mm(jnp.concatenate([start_re, start_im], 0), real_lanes) + mm(
        jnp.concatenate([-start_im, start_re], 0), imag_lanes
    )

    other_groups = pl.ds(0, groups - 1)
    arrivals = []
    total = jnp.zeros((lanes, lanes), jnp.float32)
    for part, (begin, count) in enumerate(PARTS):
        landing = spectra.at[other_groups, pl.ds(begin, count)]
        arrivals.append(block_copy(part, landing, landing, group_peers[0]))
        arrivals[part].wait_recv()
        for c in range(begin, begin + count):
            rows = spectra[:, c].reshape(lanes, width)
            total = total + mm_nt(rows, rows, None)

    tile = (ROWS, lanes)
    row_part = iota(tile, 0) // SHARE % 2
    lane_part = iota(tile, 1) // SHARE % 2

    def next_lanes(value):
        return pltpu.roll(value, lanes - SHARE, 1)

    def previous_lanes(value):
        return pltpu.roll(value, SHARE, 1)

    for t in range(groups // 4):
        packed = jnp.zeros(tile, jnp.float32)
        for slot in range(4):
            row_slot, lane_slot = slot // 2, slot % 2
            begin = (4 * t + slot) * ROWS
            value = total[begin : begin + ROWS]
            swapped = pltpu.roll(value, SHARE, 0)
            less = swapped - value if row_slot else value - swapped
            both = value + swapped
            entry = previous_lanes(less) + both if lane_slot else less + next_lanes(both)
            packed = jnp.where((row_part == row_slot) & (lane_part == lane_slot), entry, packed)
        gram_in[share, t] = packed

    def gram_copy(source, landing, peer):
        return pltpu.make_async_remote_copy(
            src_ref=source,
            dst_ref=landing,
            send_sem=gram_send,
            recv_sem=gram_recv,
            device_id=(peer, group),
            device_id_type=MESH,
        )

    for peer in share_peers:
        gram_copy(gram_in.at[share], gram_in.at[share], peer).start()
    other_shares = pl.ds(0, shares - 1)
    gram_arrivals = gram_copy(gram_in.at[other_shares], gram_in.at[other_shares], share_peers[0])
    gram_arrivals.wait_recv()
    packed = jnp.sum(gram_in[...], axis=0) * (1.0 / (COMP * width * shares))
    unpacked = []
    for t in range(groups // 4):
        value = packed[t]
        spread = [
            jnp.where(lane_part == 0, value, previous_lanes(value)),
            jnp.where(lane_part == 1, value, next_lanes(value)),
        ]
        for slot in range(4):
            row_slot, lane_slot = slot // 2, slot % 2
            value = spread[lane_slot]
            unpacked.append(jnp.where(row_part == row_slot, value, pltpu.roll(value, SHARE, 0)))
    unpacked = jnp.concatenate(unpacked, 0)
    flipped = unpacked.T
    row_part = iota((lanes, lanes), 0) // SHARE % 2
    lane_part = iota((lanes, lanes), 1) // SHARE % 2
    matrix = 0.5 * (
        jnp.where(row_part > lane_part, -unpacked, unpacked) + jnp.where(row_part < lane_part, -flipped, flipped)
    )

    nxt = mm(coef, matrix)
    image = mm(nxt, matrix)
    flat = Flat()
    for step in range(ITERS):
        rows = mm_nt(nxt, jnp.concatenate([image[:RANK]] * 8, 0))
        if step < ITERS - 1:
            further = mm(image, matrix)
        left = left_form(flat.embedded(flat.inverse_root(flat.from_rows(rows))))
        if step < ITERS - 1:
            nxt, image = wide(left, right_form(image)), wide(left, right_form(further))
        else:
            coef, final = wide(left, right_form(nxt)), wide(left, right_form(image))

    squares = mm_nt(jnp.ones((ROWS, lanes), jnp.float32), jnp.concatenate([final * final] * 4, 0))
    energy[group] = squares[:1, :]

    def energy_copy(source, landing, peer):
        return pltpu.make_async_remote_copy(
            src_ref=source,
            dst_ref=landing,
            send_sem=energy_send,
            recv_sem=energy_recv,
            device_id=(share, peer),
            device_id_type=MESH,
        )

    for peer in group_peers:
        energy_copy(energy.at[group], energy.at[group], peer).start()

    coef_low = coef.astype(jnp.bfloat16)
    inv_weight = 1.0 / root_weight
    for c in range(COMP):
        out = wide(coef_low, spectra[:, c].reshape(lanes, width)) * inv_weight
        modes[0, c] = out[:RANK]
        modes[1, c] = out[RANK:]
    store = pltpu.make_async_copy(modes, modes_hbm, store_sem)
    store.start()

    energy_copy(energy.at[other_groups], energy.at[other_groups], group_peers[0]).wait()
    energy_out[...] = energy[...].reshape(groups, 128)[:, :RANK]
    gram_arrivals.wait_send()
    for arrival in arrivals:
        arrival.wait_send()
    store.wait()


def finish(modes_in, energy_in, modes_out, energy_out, modes_sem, energy_sem):
    copies = [
        pltpu.make_async_copy(modes_in, modes_out, modes_sem),
        pltpu.make_async_copy(energy_in, energy_out, energy_sem),
    ]
    for copy in copies:
        copy.start()
    for copy in copies:
        copy.wait()


def per_device(snapshots, quadrature, omega):
    groups, shares = lax.axis_size("blk"), lax.axis_size("space")
    width = snapshots.shape[3]
    lanes = groups * ROWS
    any_space = pl.BlockSpec(memory_space=pl.ANY)
    dma = pltpu.SemaphoreType.DMA
    modes, energies = pl.pallas_call(
        functools.partial(kernel, groups, shares),
        out_shape=(
            jax.ShapeDtypeStruct((2, COMP, RANK, width), jnp.float32),
            jax.ShapeDtypeStruct((NF, RANK), jnp.float32),
        ),
        in_specs=[any_space] * 4,
        out_specs=(any_space, pl.BlockSpec(memory_space=pltpu.VMEM)),
        scratch_shapes=[
            pltpu.VMEM((COMP, SHARE * NT, width), jnp.bfloat16),
            pltpu.VMEM((2 * NF, NT), jnp.bfloat16),
            pltpu.VMEM((1, width), jnp.float32),
            pltpu.VMEM((2, RANK, groups * SHARE), jnp.float32),
            pltpu.VMEM((lanes, SHARE * NT), jnp.bfloat16),
            pltpu.VMEM((groups, COMP, ROWS, width), jnp.bfloat16),
            pltpu.VMEM((groups, COMP, ROWS, width), jnp.bfloat16),
            pltpu.VMEM((shares, groups // 4, ROWS, lanes), jnp.float32),
            pltpu.VMEM((groups, 1, 128), jnp.float32),
            pltpu.VMEM((2, COMP, RANK, width), jnp.float32),
            dma((3,)),
            dma((COMP, SHARE)),
            dma((len(PARTS),)),
            dma((len(PARTS),)),
            dma(()),
            dma(()),
            dma(()),
            dma(()),
            dma(()),
        ],
        compiler_params=pltpu.CompilerParams(
            collective_id=0, has_side_effects=True, vmem_limit_bytes=40 << 20
        ),
    )(
        *(
            pltpu.with_memory_space_constraint(operand, pltpu.HBM)
            for operand in (
                jnp.transpose(snapshots, (0, 2, 1, 3)),
                jnp.asarray(dft_table()),
                quadrature.reshape(1, width),
                jnp.transpose(omega, (0, 1, 3, 2)),
            )
        )
    )
    modes, energies = pl.pallas_call(
        finish,
        out_shape=(
            jax.ShapeDtypeStruct(modes.shape, modes.dtype),
            jax.ShapeDtypeStruct(energies.shape, energies.dtype),
        ),
        in_specs=[pl.BlockSpec(memory_space=pltpu.VMEM)] * 2,
        out_specs=(any_space, any_space),
        scratch_shapes=[dma(()), dma(())],
    )(
        pltpu.with_memory_space_constraint(modes, pltpu.VMEM),
        pltpu.with_memory_space_constraint(energies, pltpu.VMEM),
    )
    return jnp.transpose(modes, (0, 2, 1, 3))[None], energies


def solution(mesh):
    in_specs = (P("blk", None, None, "space"), P("space"), P())
    out_specs = (P("blk", None, None, None, "space"), P())
    return jax.shard_map(
        per_device, mesh=mesh, in_specs=in_specs, out_specs=out_specs, check_vma=False
    )
```

```python
import functools
import math

import jax
import jax.numpy as jnp
import numpy as np
from jax import lax
from jax.experimental import pallas as pl
from jax.experimental.pallas import tpu as pltpu
from jax.sharding import PartitionSpec as P

NT = 512
NF = 16
RANK = 16
COMP = 3
ITERS = 2
NS_STEPS = 14
SHARE = 4
ROWS = 2 * SHARE
PARTS = ((0, 1), (1, 2))
HIGHEST = lax.Precision.HIGHEST
MESH = pl.DeviceIdType.MESH


def dft_table():
    sample = np.arange(NT)
    harmonic = np.arange(1, NF + 1)
    phases = 2.0 * math.pi / NT * (harmonic[:, None] * sample[None, :] % NT)
    window = 0.5 - 0.5 * np.cos(2.0 * math.pi / NT * sample)
    factor = 1.0 / np.sqrt(np.sum(window * window))
    table = np.concatenate([window * np.cos(phases), -window * np.sin(phases)], 0) * factor
    return table.astype(np.float32).astype(jnp.bfloat16)


def far_first(count):
    return sorted(range(1, count), key=lambda step: -min(step, count - step))


def grid_far_first(side):
    offsets = [(i, j) for i in range(side) for j in range(side) if i or j]
    return sorted(offsets, key=lambda o: -min(o[0], side - o[0]) - min(o[1], side - o[1]))


def iota(shape, dim):
    return lax.broadcasted_iota(jnp.int32, shape, dim)


def mm(left, right, precision=HIGHEST):
    return jnp.dot(left, right, precision=precision, preferred_element_type=jnp.float32)


def mm_nt(left, right, precision=HIGHEST):
    return lax.dot_general(
        left, right, (((1,), (1,)), ((), ())), precision=precision, preferred_element_type=jnp.float32
    )


def pieces(value):
    high = value.astype(jnp.bfloat16).astype(jnp.float32)
    rest = value - high
    mid = rest.astype(jnp.bfloat16).astype(jnp.float32)
    return high, mid, rest - mid


def left_form(value):
    high, mid, low = pieces(value)
    lane = iota(value.shape, 1)
    near = jnp.where(lane < 96, high, mid).astype(jnp.bfloat16)
    far = jnp.where(lane < 32, mid, jnp.where(lane < 64, low, 0.0)).astype(jnp.bfloat16)
    return jnp.concatenate([near, far], axis=1)


def right_form(value):
    high, mid, low = (piece.astype(jnp.bfloat16) for piece in pieces(value))
    return jnp.concatenate([high, mid, low, high, mid, high, high, high], axis=0)


def wide(left, right):
    return jnp.dot(left, right, preferred_element_type=jnp.float32)


def lane_sum_free(value):
    for shift in (4, 2, 1):
        value = value + pltpu.roll(value, shift, 0)
    return value


def take(value, index):
    return jnp.take_along_axis(value, index, axis=1)


class Flat:
    def __init__(self):
        sub, lane = iota((8, 128), 0), iota((8, 128), 1)
        self.left_index = [lane // RANK * RANK + 8 * half + sub for half in range(2)]
        self.right_index = sub * RANK + lane % RANK
        self.own_row = lane // RANK == sub
        zero = jnp.zeros((8, 128), jnp.float32)
        self.eye = [
            jnp.where(lane // RANK + 8 * half == lane % RANK, 1.0, 0.0).astype(jnp.float32)
            for half in range(2)
        ] + [zero, zero]

    def left(self, mat):
        return [[take(entry, index) for entry in mat] for index in self.left_index]

    def right(self, mat):
        return [take(entry, self.right_index) for entry in mat]

    def product(self, left, right):
        out = []
        for p in range(2):
            for h in range(2):
                if p == 0:
                    terms = [left[k][h] * right[k] - left[k][2 + h] * right[2 + k] for k in range(2)]
                else:
                    terms = [left[k][h] * right[2 + k] + left[k][2 + h] * right[k] for k in range(2)]
                out.append(lane_sum_free(terms[0] + terms[1]))
        return out

    def from_rows(self, rows):
        return [
            lane_sum_free(jnp.where(self.own_row, rows[8 * part : 8 * part + 8], 0.0))
            for part in range(4)
        ]

    def embedded(self, mat):
        real = jnp.concatenate([take(mat[0], self.right_index), take(mat[1], self.right_index)], 0)
        imag = jnp.concatenate([take(mat[2], self.right_index), take(mat[3], self.right_index)], 0)
        first = iota((RANK, 128), 1) % (2 * RANK) < RANK
        return jnp.concatenate([jnp.where(first, real, -imag), jnp.where(first, imag, real)], 0)

    def inverse_root(self, mat):
        eye = self.eye
        left_eye, right_eye = self.left(eye), self.right(eye)

        def factor_of(one, entry):
            return 1.5 * one - 0.5 * entry

        square = sum(entry * entry for entry in mat)
        norm = jnp.sqrt(2.0 * jnp.sum(square, axis=1, keepdims=True))
        inv_norm = 1.0 / norm
        left = self.left(mat)
        squared = self.product(left, self.right(mat))
        first = [entry * inv_norm for entry in mat]
        inverse_state = [factor_of(one, entry) for one, entry in zip(eye, first)]
        partly = [1.5 * entry - 0.5 * (twice * (inv_norm * inv_norm)) for entry, twice in zip(first, squared)]
        left_factor = [[factor_of(one, entry * inv_norm) for one, entry in zip(*pair)] for pair in zip(left_eye, left)]
        both = self.product(left_factor, self.right(partly))
        for step in range(1, NS_STEPS):
            left = self.left(both)
            left_factor = [[factor_of(one, entry) for one, entry in zip(*pair)] for pair in zip(left_eye, left)]
            if step < NS_STEPS - 1:
                right_factor = [factor_of(one, entry) for one, entry in zip(right_eye, self.right(both))]
                partly = self.product(left, right_factor)
                both = self.product(left_factor, self.right(partly))
            inverse_state = self.product(left_factor, self.right(inverse_state))
        scale = 1.0 / jnp.sqrt(norm)
        return [entry * scale for entry in inverse_state]


def kernel(
    groups,
    shares,
    snap_hbm,
    table_hbm,
    quad_hbm,
    omega_hbm,
    modes_hbm,
    energy_out,
    snap,
    table,
    quad,
    omega,
    filt,
    outgoing,
    spectra,
    gram_in,
    energy,
    modes,
    small_sem,
    load_sem,
    send_sem,
    recv_sem,
    gram_send,
    gram_recv,
    energy_send,
    energy_recv,
    store_sem,
):
    group = lax.axis_index("blk")
    share = lax.axis_index("space")
    block_total = groups * SHARE
    lanes = groups * ROWS
    width = snap.shape[2]

    barrier = pltpu.get_barrier_semaphore()
    side = math.isqrt(shares)
    group_peers = [lax.rem(group + i, groups) for i in far_first(groups)]
    share_peers = [
        lax.rem(share // side + i, side) * side + lax.rem(share + j, side)
        for i, j in grid_far_first(side)
    ]
    for peer in group_peers:
        pl.semaphore_signal(barrier, inc=1, device_id=(share, peer), device_id_type=MESH)
    for peer in share_peers:
        pl.semaphore_signal(barrier, inc=1, device_id=(peer, group), device_id_type=MESH)

    small = [
        pltpu.make_async_copy(table_hbm, table, small_sem.at[0]),
        pltpu.make_async_copy(quad_hbm, quad, small_sem.at[1]),
        pltpu.make_async_copy(omega_hbm.at[group], omega, small_sem.at[2]),
    ]
    for copy in small:
        copy.start()
    loads = [
        [
            pltpu.make_async_copy(snap_hbm.at[b, c], snap.at[c, pl.ds(b * NT, NT)], load_sem.at[c, b])
            for b in range(SHARE)
        ]
        for c in range(COMP)
    ]
    for per_comp in loads:
        for copy in per_comp:
            copy.start()


    for copy in small:
        copy.wait()

    row = iota((lanes, 2 * NF), 0)
    column = iota((lanes, 2 * NF), 1)
    wanted = row // ROWS + NF * (row // SHARE % 2)
    for b in range(SHARE):
        chosen = jnp.where((column == wanted) & (row % SHARE == b), 1.0, 0.0).astype(jnp.bfloat16)
        filt[:, b * NT : (b + 1) * NT] = wide(chosen, table[...]).astype(jnp.bfloat16)
    root_weight = jnp.sqrt(quad[...])

    def block_copy(part, source, landing, peer):
        return pltpu.make_async_remote_copy(
            src_ref=source,
            dst_ref=landing,
            send_sem=send_sem.at[part],
            recv_sem=recv_sem.at[part],
            device_id=(share, peer),
            device_id_type=MESH,
        )

    for c in range(COMP):
        for copy in loads[c]:
            copy.wait()
        weighted = (wide(filt[...], snap[c]) * root_weight).astype(jnp.bfloat16)
        outgoing[:, c] = weighted.reshape(groups, ROWS, width)
        for part, (begin, count) in enumerate(PARTS):
            if c != begin + count - 1:
                continue
            if part == 0:
                pl.semaphore_wait(barrier, groups + shares - 2)
            comps = pl.ds(begin, count)
            for peer in group_peers:
                block_copy(part, outgoing.at[peer, comps], spectra.at[group, comps], peer).start()
    spectra[group] = outgoing[group]

    block = iota((block_total, lanes), 0)
    lane = iota((block_total, lanes), 1)
    same_block = block == lane // ROWS * SHARE + lane % SHARE
    is_real = lane // SHARE % 2 == 0
    real_lanes = jnp.where(same_block & is_real, 1.0, 0.0).astype(jnp.float32)
    imag_lanes = jnp.where(same_block & ~is_real, 1.0, 0.0).astype(jnp.float32)
    start_re, start_im = omega[0], omega[1]
    coef = mm(jnp.concatenate([start_re, start_im], 0), real_lanes) + mm(
        jnp.concatenate([-start_im, start_re], 0), imag_lanes
    )

    other_groups = pl.ds(0, groups - 1)
    arrivals = []
    total = jnp.zeros((lanes, lanes), jnp.float32)
    for part, (begin, count) in enumerate(PARTS):
        landing = spectra.at[other_groups, pl.ds(begin, count)]
        arrivals.append(block_copy(part, landing, landing, group_peers[0]))
        arrivals[part].wait_recv()
        for c in range(begin, begin + count):
            rows = spectra[:, c].reshape(lanes, width)
            total = total + mm_nt(rows, rows, None)

    tile = (ROWS, lanes)
    row_part = iota(tile, 0) // SHARE % 2
    lane_part = iota(tile, 1) // SHARE % 2

    def next_lanes(value):
        return pltpu.roll(value, lanes - SHARE, 1)

    def previous_lanes(value):
        return pltpu.roll(value, SHARE, 1)

    for t in range(groups // 4):
        packed = jnp.zeros(tile, jnp.float32)
        for slot in range(4):
            row_slot, lane_slot = slot // 2, slot % 2
            begin = (4 * t + slot) * ROWS
            value = total[begin : begin + ROWS]
            swapped = pltpu.roll(value, SHARE, 0)
            less = swapped - value if row_slot else value - swapped
            both = value + swapped
            entry = previous_lanes(less) + both if lane_slot else less + next_lanes(both)
            packed = jnp.where((row_part == row_slot) & (lane_part == lane_slot), entry, packed)
        gram_in[share, t] = packed

    def gram_copy(source, landing, peer):
        return pltpu.make_async_remote_copy(
            src_ref=source,
            dst_ref=landing,
            send_sem=gram_send,
            recv_sem=gram_recv,
            device_id=(peer, group),
            device_id_type=MESH,
        )

    for peer in share_peers:
        gram_copy(gram_in.at[share], gram_in.at[share], peer).start()
    other_shares = pl.ds(0, shares - 1)
    gram_arrivals = gram_copy(gram_in.at[other_shares], gram_in.at[other_shares], share_peers[0])
    gram_arrivals.wait_recv()
    packed = jnp.sum(gram_in[...], axis=0) * (1.0 / (COMP * width * shares))
    unpacked = []
    for t in range(groups // 4):
        value = packed[t]
        spread = [
            jnp.where(lane_part == 0, value, previous_lanes(value)),
            jnp.where(lane_part == 1, value, next_lanes(value)),
        ]
        for slot in range(4):
            row_slot, lane_slot = slot // 2, slot % 2
            value = spread[lane_slot]
            unpacked.append(jnp.where(row_part == row_slot, value, pltpu.roll(value, SHARE, 0)))
    unpacked = jnp.concatenate(unpacked, 0)
    flipped = unpacked.T
    row_part = iota((lanes, lanes), 0) // SHARE % 2
    lane_part = iota((lanes, lanes), 1) // SHARE % 2
    matrix = 0.5 * (
        jnp.where(row_part > lane_part, -unpacked, unpacked) + jnp.where(row_part < lane_part, -flipped, flipped)
    )

    nxt = mm(coef, matrix)
    image = mm(nxt, matrix)
    flat = Flat()

    def inner(first, second):
        return flat.from_rows(mm_nt(first, jnp.concatenate([second[:RANK]] * 8, 0)))

    small = inner(nxt, image)
    for step in range(ITERS):
        if step < ITERS - 1:
            further = mm(image, matrix)
            ahead = inner(image, further)
        root = flat.inverse_root(small)
        left = left_form(flat.embedded(root))
        if step < ITERS - 1:
            small = flat.product(flat.left(root), flat.right(ahead))
            small = flat.product(flat.left(small), flat.right(root))
            nxt, image = wide(left, right_form(image)), wide(left, right_form(further))
        else:
            coef, final = wide(left, right_form(nxt)), wide(left, right_form(image))

    squares = mm_nt(jnp.ones((ROWS, lanes), jnp.float32), jnp.concatenate([final * final] * 4, 0))
    energy[group] = squares[:1, :]

    def energy_copy(source, landing, peer):
        return pltpu.make_async_remote_copy(
            src_ref=source,
            dst_ref=landing,
            send_sem=energy_send,
            recv_sem=energy_recv,
            device_id=(share, peer),
            device_id_type=MESH,
        )

    for peer in group_peers:
        energy_copy(energy.at[group], energy.at[group], peer).start()

    coef_low = coef.astype(jnp.bfloat16)
    inv_weight = 1.0 / root_weight
    for c in range(COMP):
        out = wide(coef_low, spectra[:, c].reshape(lanes, width)) * inv_weight
        modes[0, c] = out[:RANK]
        modes[1, c] = out[RANK:]
    store = pltpu.make_async_copy(modes, modes_hbm, store_sem)
    store.start()

    energy_copy(energy.at[other_groups], energy.at[other_groups], group_peers[0]).wait()
    energy_out[...] = energy[...].reshape(groups, 128)[:, :RANK]
    gram_arrivals.wait_send()
    for arrival in arrivals:
        arrival.wait_send()
    store.wait()


def finish(modes_in, energy_in, modes_out, energy_out, modes_sem, energy_sem):
    copies = [
        pltpu.make_async_copy(modes_in, modes_out, modes_sem),
        pltpu.make_async_copy(energy_in, energy_out, energy_sem),
    ]
    for copy in copies:
        copy.start()
    for copy in copies:
        copy.wait()


def per_device(snapshots, quadrature, omega):
    groups, shares = lax.axis_size("blk"), lax.axis_size("space")
    width = snapshots.shape[3]
    lanes = groups * ROWS
    any_space = pl.BlockSpec(memory_space=pl.ANY)
    dma = pltpu.SemaphoreType.DMA
    modes, energies = pl.pallas_call(
        functools.partial(kernel, groups, shares),
        out_shape=(
            jax.ShapeDtypeStruct((2, COMP, RANK, width), jnp.float32),
            jax.ShapeDtypeStruct((NF, RANK), jnp.float32),
        ),
        in_specs=[any_space] * 4,
        out_specs=(any_space, pl.BlockSpec(memory_space=pltpu.VMEM)),
        scratch_shapes=[
            pltpu.VMEM((COMP, SHARE * NT, width), jnp.bfloat16),
            pltpu.VMEM((2 * NF, NT), jnp.bfloat16),
            pltpu.VMEM((1, width), jnp.float32),
            pltpu.VMEM((2, RANK, groups * SHARE), jnp.float32),
            pltpu.VMEM((lanes, SHARE * NT), jnp.bfloat16),
            pltpu.VMEM((groups, COMP, ROWS, width), jnp.bfloat16),
            pltpu.VMEM((groups, COMP, ROWS, width), jnp.bfloat16),
            pltpu.VMEM((shares, groups // 4, ROWS, lanes), jnp.float32),
            pltpu.VMEM((groups, 1, 128), jnp.float32),
            pltpu.VMEM((2, COMP, RANK, width), jnp.float32),
            dma((3,)),
            dma((COMP, SHARE)),
            dma((len(PARTS),)),
            dma((len(PARTS),)),
            dma(()),
            dma(()),
            dma(()),
            dma(()),
            dma(()),
        ],
        compiler_params=pltpu.CompilerParams(
            collective_id=0, has_side_effects=True, vmem_limit_bytes=40 << 20
        ),
    )(
        *(
            pltpu.with_memory_space_constraint(operand, pltpu.HBM)
            for operand in (
                jnp.transpose(snapshots, (0, 2, 1, 3)),
                jnp.asarray(dft_table()),
                quadrature.reshape(1, width),
                jnp.transpose(omega, (0, 1, 3, 2)),
            )
        )
    )
    modes, energies = pl.pallas_call(
        finish,
        out_shape=(
            jax.ShapeDtypeStruct(modes.shape, modes.dtype),
            jax.ShapeDtypeStruct(energies.shape, energies.dtype),
        ),
        in_specs=[pl.BlockSpec(memory_space=pltpu.VMEM)] * 2,
        out_specs=(any_space, any_space),
        scratch_shapes=[dma(()), dma(())],
    )(
        pltpu.with_memory_space_constraint(modes, pltpu.VMEM),
        pltpu.with_memory_space_constraint(energies, pltpu.VMEM),
    )
    return jnp.transpose(modes, (0, 2, 1, 3))[None], energies


def solution(mesh):
    in_specs = (P("blk", None, None, "space"), P("space"), P())
    out_specs = (P("blk", None, None, None, "space"), P())
    return jax.shard_map(
        per_device, mesh=mesh, in_specs=in_specs, out_specs=out_specs, check_vma=False
    )
```

```python
import functools
import math

import jax
import jax.numpy as jnp
import numpy as np
from jax import lax
from jax.experimental import pallas as pl
from jax.experimental.pallas import tpu as pltpu
from jax.sharding import PartitionSpec as P

NT = 512
NF = 16
RANK = 16
COMP = 3
ITERS = 2
NS_STEPS = 14
SHARE = 4
ROWS = 2 * SHARE
LEFT_ORDER = (0, 0, 0, 1, 1, 2)
RIGHT_ORDER = (0, 1, 2, 0, 1, 0)
PARTS = ((0, 1), (1, 2))
HIGHEST = lax.Precision.HIGHEST
MESH = pl.DeviceIdType.MESH


def dft_table():
    sample = np.arange(NT)
    harmonic = np.arange(1, NF + 1)
    phases = 2.0 * math.pi / NT * (harmonic[:, None] * sample[None, :] % NT)
    window = 0.5 - 0.5 * np.cos(2.0 * math.pi / NT * sample)
    factor = 1.0 / np.sqrt(np.sum(window * window))
    table = np.concatenate([window * np.cos(phases), -window * np.sin(phases)], 0) * factor
    return table.astype(np.float32).astype(jnp.bfloat16)


def far_first(count):
    return sorted(range(1, count), key=lambda step: -min(step, count - step))


def grid_far_first(side):
    offsets = [(i, j) for i in range(side) for j in range(side) if i or j]
    return sorted(offsets, key=lambda o: -min(o[0], side - o[0]) - min(o[1], side - o[1]))


def iota(shape, dim):
    return lax.broadcasted_iota(jnp.int32, shape, dim)


def mm(left, right, precision=HIGHEST):
    return jnp.dot(left, right, precision=precision, preferred_element_type=jnp.float32)


def mm_nt(left, right, precision=HIGHEST):
    return lax.dot_general(
        left, right, (((1,), (1,)), ((), ())), precision=precision, preferred_element_type=jnp.float32
    )


def pieces(value):
    high = value.astype(jnp.bfloat16).astype(jnp.float32)
    rest = value - high
    mid = rest.astype(jnp.bfloat16).astype(jnp.float32)
    return high, mid, rest - mid


def left_form(value):
    high, mid, low = pieces(value)
    lane = iota(value.shape, 1)
    near = jnp.where(lane < 96, high, mid).astype(jnp.bfloat16)
    far = jnp.where(lane < 32, mid, jnp.where(lane < 64, low, 0.0)).astype(jnp.bfloat16)
    return jnp.concatenate([near, far], axis=1)


def right_form(value):
    high, mid, low = (piece.astype(jnp.bfloat16) for piece in pieces(value))
    return jnp.concatenate([high, mid, low, high, mid, high, high, high], axis=0)


def lane_form(value, order):
    parts = [piece.astype(jnp.bfloat16) for piece in pieces(value)]
    return jnp.concatenate([parts[i] for i in order], axis=1)


def sublane_form(value, order):
    parts = [piece.astype(jnp.bfloat16) for piece in pieces(value)]
    return jnp.concatenate([parts[i] for i in order], axis=0)


def wide(left, right):
    return jnp.dot(left, right, preferred_element_type=jnp.float32)


def lane_sum_free(value):
    for shift in (4, 2, 1):
        value = value + pltpu.roll(value, shift, 0)
    return value


def take(value, index):
    return jnp.take_along_axis(value, index, axis=1)


class Flat:
    def __init__(self):
        sub, lane = iota((8, 128), 0), iota((8, 128), 1)
        self.left_index = [lane // RANK * RANK + 8 * half + sub for half in range(2)]
        self.right_index = sub * RANK + lane % RANK
        self.own_row = lane // RANK == sub
        zero = jnp.zeros((8, 128), jnp.float32)
        self.eye = [
            jnp.where(lane // RANK + 8 * half == lane % RANK, 1.0, 0.0).astype(jnp.float32)
            for half in range(2)
        ] + [zero, zero]

    def left(self, mat):
        return [[take(entry, index) for entry in mat] for index in self.left_index]

    def right(self, mat):
        return [take(entry, self.right_index) for entry in mat]

    def product(self, left, right):
        out = []
        for p in range(2):
            for h in range(2):
                if p == 0:
                    terms = [left[k][h] * right[k] - left[k][2 + h] * right[2 + k] for k in range(2)]
                else:
                    terms = [left[k][h] * right[2 + k] + left[k][2 + h] * right[k] for k in range(2)]
                out.append(lane_sum_free(terms[0] + terms[1]))
        return out

    def from_rows(self, rows):
        return [
            lane_sum_free(jnp.where(self.own_row, rows[8 * part : 8 * part + 8], 0.0))
            for part in range(4)
        ]

    def embedded(self, mat):
        real = jnp.concatenate([take(mat[0], self.right_index), take(mat[1], self.right_index)], 0)
        imag = jnp.concatenate([take(mat[2], self.right_index), take(mat[3], self.right_index)], 0)
        first = iota((RANK, 128), 1) % (2 * RANK) < RANK
        return jnp.concatenate([jnp.where(first, real, -imag), jnp.where(first, imag, real)], 0)

    def inverse_root(self, mat):
        eye = self.eye
        left_eye, right_eye = self.left(eye), self.right(eye)

        def factor_of(one, entry):
            return 1.5 * one - 0.5 * entry

        square = sum(entry * entry for entry in mat)
        norm = jnp.sqrt(2.0 * jnp.sum(square, axis=1, keepdims=True))
        inv_norm = 1.0 / norm
        left = self.left(mat)
        squared = self.product(left, self.right(mat))
        first = [entry * inv_norm for entry in mat]
        inverse_state = [factor_of(one, entry) for one, entry in zip(eye, first)]
        partly = [1.5 * entry - 0.5 * (twice * (inv_norm * inv_norm)) for entry, twice in zip(first, squared)]
        left_factor = [[factor_of(one, entry * inv_norm) for one, entry in zip(*pair)] for pair in zip(left_eye, left)]
        both = self.product(left_factor, self.right(partly))
        for step in range(1, NS_STEPS):
            left = self.left(both)
            left_factor = [[factor_of(one, entry) for one, entry in zip(*pair)] for pair in zip(left_eye, left)]
            if step < NS_STEPS - 1:
                right_factor = [factor_of(one, entry) for one, entry in zip(right_eye, self.right(both))]
                partly = self.product(left, right_factor)
                both = self.product(left_factor, self.right(partly))
            inverse_state = self.product(left_factor, self.right(inverse_state))
        scale = 1.0 / jnp.sqrt(norm)
        return [entry * scale for entry in inverse_state]


def kernel(
    groups,
    shares,
    snap_hbm,
    table_hbm,
    quad_hbm,
    omega_hbm,
    modes_hbm,
    energy_out,
    snap,
    table,
    quad,
    omega,
    filt,
    outgoing,
    spectra,
    gram_in,
    energy,
    modes,
    small_sem,
    load_sem,
    send_sem,
    recv_sem,
    gram_send,
    gram_recv,
    energy_send,
    energy_recv,
    store_sem,
):
    group = lax.axis_index("blk")
    share = lax.axis_index("space")
    block_total = groups * SHARE
    lanes = groups * ROWS
    width = snap.shape[2]

    barrier = pltpu.get_barrier_semaphore()
    side = math.isqrt(shares)
    group_peers = [lax.rem(group + i, groups) for i in far_first(groups)]
    share_peers = [
        lax.rem(share // side + i, side) * side + lax.rem(share + j, side)
        for i, j in grid_far_first(side)
    ]
    for peer in group_peers:
        pl.semaphore_signal(barrier, inc=1, device_id=(share, peer), device_id_type=MESH)
    for peer in share_peers:
        pl.semaphore_signal(barrier, inc=1, device_id=(peer, group), device_id_type=MESH)

    small = [
        pltpu.make_async_copy(table_hbm, table, small_sem.at[0]),
        pltpu.make_async_copy(quad_hbm, quad, small_sem.at[1]),
        pltpu.make_async_copy(omega_hbm.at[group], omega, small_sem.at[2]),
    ]
    for copy in small:
        copy.start()
    loads = [
        [
            pltpu.make_async_copy(snap_hbm.at[b, c], snap.at[c, pl.ds(b * NT, NT)], load_sem.at[c, b])
            for b in range(SHARE)
        ]
        for c in range(COMP)
    ]
    for per_comp in loads:
        for copy in per_comp:
            copy.start()


    for copy in small:
        copy.wait()

    row = iota((lanes, 2 * NF), 0)
    column = iota((lanes, 2 * NF), 1)
    wanted = row // ROWS + NF * (row // SHARE % 2)
    for b in range(SHARE):
        chosen = jnp.where((column == wanted) & (row % SHARE == b), 1.0, 0.0).astype(jnp.bfloat16)
        filt[:, b * NT : (b + 1) * NT] = wide(chosen, table[...]).astype(jnp.bfloat16)
    root_weight = jnp.sqrt(quad[...])

    def block_copy(part, source, landing, peer):
        return pltpu.make_async_remote_copy(
            src_ref=source,
            dst_ref=landing,
            send_sem=send_sem.at[part],
            recv_sem=recv_sem.at[part],
            device_id=(share, peer),
            device_id_type=MESH,
        )

    for c in range(COMP):
        for copy in loads[c]:
            copy.wait()
        weighted = (wide(filt[...], snap[c]) * root_weight).astype(jnp.bfloat16)
        outgoing[:, c] = weighted.reshape(groups, ROWS, width)
        for part, (begin, count) in enumerate(PARTS):
            if c != begin + count - 1:
                continue
            if part == 0:
                pl.semaphore_wait(barrier, groups + shares - 2)
            comps = pl.ds(begin, count)
            for peer in group_peers:
                block_copy(part, outgoing.at[peer, comps], spectra.at[group, comps], peer).start()
    spectra[group] = outgoing[group]

    block = iota((block_total, lanes), 0)
    lane = iota((block_total, lanes), 1)
    same_block = block == lane // ROWS * SHARE + lane % SHARE
    is_real = lane // SHARE % 2 == 0
    real_lanes = jnp.where(same_block & is_real, 1.0, 0.0).astype(jnp.float32)
    imag_lanes = jnp.where(same_block & ~is_real, 1.0, 0.0).astype(jnp.float32)
    start_re, start_im = omega[0], omega[1]
    coef = mm(jnp.concatenate([start_re, start_im], 0), real_lanes) + mm(
        jnp.concatenate([-start_im, start_re], 0), imag_lanes
    )

    other_groups = pl.ds(0, groups - 1)
    arrivals = []
    total = jnp.zeros((lanes, lanes), jnp.float32)
    for part, (begin, count) in enumerate(PARTS):
        landing = spectra.at[other_groups, pl.ds(begin, count)]
        arrivals.append(block_copy(part, landing, landing, group_peers[0]))
        arrivals[part].wait_recv()
        for c in range(begin, begin + count):
            rows = spectra[:, c].reshape(lanes, width)
            total = total + mm_nt(rows, rows, None)

    tile = (ROWS, lanes)
    row_part = iota(tile, 0) // SHARE % 2
    lane_part = iota(tile, 1) // SHARE % 2

    def next_lanes(value):
        return pltpu.roll(value, lanes - SHARE, 1)

    def previous_lanes(value):
        return pltpu.roll(value, SHARE, 1)

    for t in range(groups // 4):
        packed = jnp.zeros(tile, jnp.float32)
        for slot in range(4):
            row_slot, lane_slot = slot // 2, slot % 2
            begin = (4 * t + slot) * ROWS
            value = total[begin : begin + ROWS]
            swapped = pltpu.roll(value, SHARE, 0)
            less = swapped - value if row_slot else value - swapped
            both = value + swapped
            entry = previous_lanes(less) + both if lane_slot else less + next_lanes(both)
            packed = jnp.where((row_part == row_slot) & (lane_part == lane_slot), entry, packed)
        gram_in[share, t] = packed

    def gram_copy(source, landing, peer):
        return pltpu.make_async_remote_copy(
            src_ref=source,
            dst_ref=landing,
            send_sem=gram_send,
            recv_sem=gram_recv,
            device_id=(peer, group),
            device_id_type=MESH,
        )

    for peer in share_peers:
        gram_copy(gram_in.at[share], gram_in.at[share], peer).start()
    other_shares = pl.ds(0, shares - 1)
    gram_arrivals = gram_copy(gram_in.at[other_shares], gram_in.at[other_shares], share_peers[0])
    gram_arrivals.wait_recv()
    packed = jnp.sum(gram_in[...], axis=0) * (1.0 / (COMP * width * shares))
    unpacked = []
    for t in range(groups // 4):
        value = packed[t]
        spread = [
            jnp.where(lane_part == 0, value, previous_lanes(value)),
            jnp.where(lane_part == 1, value, next_lanes(value)),
        ]
        for slot in range(4):
            row_slot, lane_slot = slot // 2, slot % 2
            value = spread[lane_slot]
            unpacked.append(jnp.where(row_part == row_slot, value, pltpu.roll(value, SHARE, 0)))
    unpacked = jnp.concatenate(unpacked, 0)
    flipped = unpacked.T
    row_part = iota((lanes, lanes), 0) // SHARE % 2
    lane_part = iota((lanes, lanes), 1) // SHARE % 2
    matrix = 0.5 * (
        jnp.where(row_part > lane_part, -unpacked, unpacked) + jnp.where(row_part < lane_part, -flipped, flipped)
    )

    wide_matrix = sublane_form(matrix, RIGHT_ORDER)
    nxt = wide(lane_form(coef, LEFT_ORDER), wide_matrix)
    image = wide(lane_form(nxt, LEFT_ORDER), wide_matrix)
    flat = Flat()

    def inner(first, second):
        return flat.from_rows(
            mm_nt(lane_form(first, LEFT_ORDER), jnp.concatenate([lane_form(second[:RANK], RIGHT_ORDER)] * 8, 0), None)
        )

    small = inner(nxt, image)
    for step in range(ITERS):
        if step < ITERS - 1:
            further = wide(lane_form(image, LEFT_ORDER), wide_matrix)
            ahead = inner(image, further)
        else:
            level = inner(image, image)
        root = flat.inverse_root(small)
        left = left_form(flat.embedded(root))
        if step < ITERS - 1:
            small = flat.product(flat.left(root), flat.right(ahead))
            small = flat.product(flat.left(small), flat.right(root))
            nxt, image = wide(left, right_form(image)), wide(left, right_form(further))
        else:
            coef = wide(left, right_form(nxt))

    rotated = flat.product(flat.left(root), flat.right(level))
    summand = [rotated[h] * root[h] + rotated[2 + h] * root[2 + h] for h in range(2)]
    lane, column = iota((128, 128), 0), iota((128, 128), 1)
    squares = sum(
        mm(summand[h], jnp.where(lane // RANK + 8 * h == column, 1.0, 0.0).astype(jnp.float32)) for h in range(2)
    )
    energy[group] = squares[:1, :]

    def energy_copy(source, landing, peer):
        return pltpu.make_async_remote_copy(
            src_ref=source,
            dst_ref=landing,
            send_sem=energy_send,
            recv_sem=energy_recv,
            device_id=(share, peer),
            device_id_type=MESH,
        )

    for peer in group_peers:
        energy_copy(energy.at[group], energy.at[group], peer).start()

    coef_low = coef.astype(jnp.bfloat16)
    inv_weight = 1.0 / root_weight
    for c in range(COMP):
        out = wide(coef_low, spectra[:, c].reshape(lanes, width)) * inv_weight
        modes[0, c] = out[:RANK]
        modes[1, c] = out[RANK:]
    store = pltpu.make_async_copy(modes, modes_hbm, store_sem)
    store.start()

    energy_copy(energy.at[other_groups], energy.at[other_groups], group_peers[0]).wait()
    energy_out[...] = energy[...].reshape(groups, 128)[:, :RANK]
    gram_arrivals.wait_send()
    for arrival in arrivals:
        arrival.wait_send()
    store.wait()


def finish(modes_in, energy_in, modes_out, energy_out, modes_sem, energy_sem):
    copies = [
        pltpu.make_async_copy(modes_in, modes_out, modes_sem),
        pltpu.make_async_copy(energy_in, energy_out, energy_sem),
    ]
    for copy in copies:
        copy.start()
    for copy in copies:
        copy.wait()


def per_device(snapshots, quadrature, omega):
    groups, shares = lax.axis_size("blk"), lax.axis_size("space")
    width = snapshots.shape[3]
    lanes = groups * ROWS
    any_space = pl.BlockSpec(memory_space=pl.ANY)
    dma = pltpu.SemaphoreType.DMA
    modes, energies = pl.pallas_call(
        functools.partial(kernel, groups, shares),
        out_shape=(
            jax.ShapeDtypeStruct((2, COMP, RANK, width), jnp.float32),
            jax.ShapeDtypeStruct((NF, RANK), jnp.float32),
        ),
        in_specs=[any_space] * 4,
        out_specs=(any_space, pl.BlockSpec(memory_space=pltpu.VMEM)),
        scratch_shapes=[
            pltpu.VMEM((COMP, SHARE * NT, width), jnp.bfloat16),
            pltpu.VMEM((2 * NF, NT), jnp.bfloat16),
            pltpu.VMEM((1, width), jnp.float32),
            pltpu.VMEM((2, RANK, groups * SHARE), jnp.float32),
            pltpu.VMEM((lanes, SHARE * NT), jnp.bfloat16),
            pltpu.VMEM((groups, COMP, ROWS, width), jnp.bfloat16),
            pltpu.VMEM((groups, COMP, ROWS, width), jnp.bfloat16),
            pltpu.VMEM((shares, groups // 4, ROWS, lanes), jnp.float32),
            pltpu.VMEM((groups, 1, 128), jnp.float32),
            pltpu.VMEM((2, COMP, RANK, width), jnp.float32),
            dma((3,)),
            dma((COMP, SHARE)),
            dma((len(PARTS),)),
            dma((len(PARTS),)),
            dma(()),
            dma(()),
            dma(()),
            dma(()),
            dma(()),
        ],
        compiler_params=pltpu.CompilerParams(
            collective_id=0, has_side_effects=True, vmem_limit_bytes=40 << 20
        ),
    )(
        *(
            pltpu.with_memory_space_constraint(operand, pltpu.HBM)
            for operand in (
                jnp.transpose(snapshots, (0, 2, 1, 3)),
                jnp.asarray(dft_table()),
                quadrature.reshape(1, width),
                jnp.transpose(omega, (0, 1, 3, 2)),
            )
        )
    )
    modes, energies = pl.pallas_call(
        finish,
        out_shape=(
            jax.ShapeDtypeStruct(modes.shape, modes.dtype),
            jax.ShapeDtypeStruct(energies.shape, energies.dtype),
        ),
        in_specs=[pl.BlockSpec(memory_space=pltpu.VMEM)] * 2,
        out_specs=(any_space, any_space),
        scratch_shapes=[dma(()), dma(())],
    )(
        pltpu.with_memory_space_constraint(modes, pltpu.VMEM),
        pltpu.with_memory_space_constraint(energies, pltpu.VMEM),
    )
    return jnp.transpose(modes, (0, 2, 1, 3))[None], energies


def solution(mesh):
    in_specs = (P("blk", None, None, "space"), P("space"), P())
    out_specs = (P("blk", None, None, None, "space"), P())
    return jax.shard_map(
        per_device, mesh=mesh, in_specs=in_specs, out_specs=out_specs, check_vma=False
    )
```
